32 devices in a mesh: row: 8 (over z, core), col: 4 (over y, x).
Axes of the slice: x: 2, y: 2, z: 4, core: 2. Of those that a mesh axis runs over, the one named last changes fastest.
Arguments:
- features: bfloat16 [9, 1, 128, 128, 128], P(None, None, 'row', 'col'), may hold values from -12 to 12
- cotangent: float32 [3, 1, 128, 128, 128], P(None, None, 'row', 'col'), may hold values from -14 to 14
- w_in: bfloat16 [9, 256], replicated, may hold values from -2 to 2
- bias_in: float32 [256], replicated, may hold values from -3 to 3
- w_mid: bfloat16 [256, 256], replicated, may hold values from -0.375 to 0.375
- bias_mid: float32 [256], replicated, may hold values from -3 to 3
- w_out: bfloat16 [256, 6], replicated, may hold values from -2.5 to 2.5
Outputs:
- grad_features: float32 [9, 1, 128, 128, 128], P(None, None, 'row', 'col')
- grad_w_in: float32 [9, 256], replicated
- grad_b_in: float32 [256], replicated
- grad_w_mid: float32 [256, 256], replicated
- grad_b_mid: float32 [256], replicated
- grad_w_out: float32 [256, 6], replicated
The draws below stay inside these ranges and needn't reach their ends.
All inputs are finite; a program needn't handle non-finite values.
Results may differ from the reference program's by a relative error of at most 0.025.
Values sent between devices are 32-bit elements; how exact they have to be, the bound alone decides.
A program may use at most 128 MiB of HBM per device.

```python
import math
import jax
import jax.numpy as jnp
from jax import lax

NX = 128
NY = 128
NZ = 128
FEAT = 9
HID = 256
OUT = 6
SAMPLES = 1
CELLS = 2097152


def draw_features(key, part):
    shape = (FEAT, SAMPLES, NX, NY, NZ)
    base_key = jax.random.fold_in(key, 11)
    scale_key = jax.random.fold_in(key, 12)
    spread = jnp.exp(jax.random.uniform(scale_key, shape, jnp.float32, math.log(0.3), math.log(3.0)))
    base = jnp.clip(jax.random.normal(base_key, shape, jnp.float32), -4.0, 4.0)
    return (base * spread).astype(jnp.bfloat16)


def draw_cotangent(key, part):
    shape = (3, SAMPLES, NX, NY, NZ)
    base_key = jax.random.fold_in(key, 21)
    scale_key = jax.random.fold_in(key, 22)
    spread = jnp.exp(jax.random.uniform(scale_key, shape, jnp.float32, math.log(0.3), math.log(3.0)))
    base = jnp.clip(jax.random.normal(base_key, shape, jnp.float32), -4.0, 4.0) * spread
    return base.astype(jnp.float32)


def scatter_about(key, shape, width, most, held_as=jnp.bfloat16):
    result = width * jax.random.normal(key, shape, jnp.float32)
    return jnp.clip(result, min=-most, max=most).astype(held_as)


def setup_inputs(seed: int = 0) -> dict:
    key_of = jax.random.split(jax.random.key(seed), 8)
    features = draw_features(jax.random.fold_in(key_of[7], 71), 0)
    cotangent = draw_cotangent(jax.random.fold_in(key_of[7], 71), 0)
    w_in = scatter_about(key_of[2], (FEAT, HID), FEAT ** -0.5, 2.0)
    bias_in = scatter_about(key_of[3], (HID,), 0.5, 3.0, jnp.float32)
    w_mid = scatter_about(key_of[4], (HID, HID), HID ** -0.5, 0.375)
    bias_mid = scatter_about(key_of[5], (HID,), 0.5, 3.0, jnp.float32)
    w_out = scatter_about(key_of[6], (HID, OUT), OUT ** -0.5, 2.5)
    return dict(features=features, cotangent=cotangent, w_in=w_in, bias_in=bias_in, w_mid=w_mid, bias_mid=bias_mid, w_out=w_out)


STEP_DT = 0.04
PAIRS = ((0, 0), (1, 1), (2, 2), (0, 1), (0, 2), (1, 2))

def integer_modes(length):
    index = jnp.arange(length, dtype=jnp.int32)
    return jnp.where(index < length // 2, index, index - length)

def stress_adjoint(cotangent):
    spectra = jnp.fft.fftn(cotangent, axes=(2, 3, 4))
    modes_x = integer_modes(NX)[:, None, None]
    modes_y = integer_modes(NY)[None, :, None]
    modes_z = integer_modes(NZ)[None, None, :]
    keep = (3 * jnp.abs(modes_x) < NX) & (3 * jnp.abs(modes_y) < NY) & (3 * jnp.abs(modes_z) < NZ)
    waves = [modes_x.astype(jnp.float32), modes_y.astype(jnp.float32), modes_z.astype(jnp.float32)]
    inner = waves[0] * spectra[0] + waves[1] * spectra[1] + waves[2] * spectra[2]
    square = jnp.maximum(waves[0] * waves[0] + waves[1] * waves[1] + waves[2] * waves[2], 1.0)
    projected = [jnp.where(keep, spectra[comp] - waves[comp] * inner / square, 0.0) for comp in range(3)]
    pieces = []
    for first, second in PAIRS:
        if first == second:
            value = waves[first] * projected[first]
        else:
            value = waves[second] * projected[first] + waves[first] * projected[second]
        pieces.append(1j * STEP_DT * value)
    stress_hat = jnp.stack(pieces)
    return jnp.real(jnp.fft.ifftn(stress_hat, axes=(2, 3, 4))).astype(jnp.float32)

def closure_block(x_blk, g_blk, w_in, bias_in, w_mid, bias_mid, w_out):
    pre_in = jnp.dot(w_in.T, x_blk, preferred_element_type=jnp.float32) + bias_in[:, None]
    act_in = jnp.tanh(pre_in).astype(jnp.bfloat16)
    pre_mid = jnp.dot(w_mid.T, act_in, preferred_element_type=jnp.float32) + bias_mid[:, None]
    act_mid = jnp.tanh(pre_mid).astype(jnp.bfloat16)
    back_mid = jnp.dot(w_out, g_blk, preferred_element_type=jnp.float32)
    delta_mid = (back_mid * (1.0 - jnp.square(act_mid.astype(jnp.float32)))).astype(jnp.bfloat16)
    back_in = jnp.dot(w_mid, delta_mid, preferred_element_type=jnp.float32)
    delta_in = (back_in * (1.0 - jnp.square(act_in.astype(jnp.float32)))).astype(jnp.bfloat16)
    grad_x = jnp.dot(w_in, delta_in, preferred_element_type=jnp.float32)
    gw_out = jnp.dot(act_mid, g_blk.T, preferred_element_type=jnp.float32)
    gw_mid = jnp.dot(act_in, delta_mid.T, preferred_element_type=jnp.float32)
    gw_in = jnp.dot(x_blk, delta_in.T, preferred_element_type=jnp.float32)
    gb_mid = lax.optimization_barrier(jnp.sum(delta_mid.astype(jnp.float32), axis=1))
    gb_in = lax.optimization_barrier(jnp.sum(delta_in.astype(jnp.float32), axis=1))
    return (grad_x, (gw_in, gb_in, gw_mid, gb_mid, gw_out))

def reference(features, cotangent, w_in, bias_in, w_mid, bias_mid, w_out):
    stress = stress_adjoint(cotangent)
    grads = stress.astype(jnp.bfloat16).reshape(OUT, CELLS)
    feats = features.reshape(FEAT, CELLS)
    block = math.gcd(CELLS, 16384)
    count = CELLS // block

    def visit(carry, index):
        start = (index * block).astype(jnp.int32)
        x_blk = lax.dynamic_slice_in_dim(feats, start, block, 1)
        g_blk = lax.dynamic_slice_in_dim(grads, start, block, 1)
        grad_x, parts = closure_block(x_blk, g_blk, w_in, bias_in, w_mid, bias_mid, w_out)
        return (tuple((a + b for a, b in zip(carry, parts))), grad_x)
    init = (jnp.zeros((FEAT, HID), jnp.float32), jnp.zeros((HID,), jnp.float32), jnp.zeros((HID, HID), jnp.float32), jnp.zeros((HID,), jnp.float32), jnp.zeros((HID, OUT), jnp.float32))
    totals, pieces = lax.scan(visit, init, jnp.arange(count, dtype=jnp.int32))
    grad_features = jnp.moveaxis(pieces, 0, 1).reshape(FEAT, SAMPLES, NX, NY, NZ)
    factor = 1.0 / math.sqrt(CELLS)
    return (grad_features, totals[0] * factor, totals[1] * factor, totals[2] * factor, totals[3] * factor, totals[4] * factor)
```

```python
import functools
import math

import jax
import jax.numpy as jnp
import numpy as np
from jax import lax
from jax.experimental import pallas as pl
from jax.experimental.pallas import tpu as pltpu
from jax.sharding import PartitionSpec as P

STEP_DT = 0.04
MESH = pl.DeviceIdType.MESH
HIGHEST = lax.Precision.HIGHEST


def kept_modes(length):
    top = (length - 1) // 3
    return top


def padded(values, parts):
    share = -(-len(values) // parts)
    out = np.zeros((parts * share,), np.int64)
    out[: len(values)] = values
    live = np.zeros((parts * share,), np.float64)
    live[: len(values)] = 1.0
    return out.reshape(parts, share), live.reshape(parts, share)


def angles(modes, length):
    pos = np.arange(length)
    turns = (modes[..., None] * pos) % length
    return turns * (2.0 * math.pi / length)


def forward_complex(modes, live, length):
    a = angles(modes, length)
    c, s = np.cos(a) * live[..., None], np.sin(a) * live[..., None]
    return np.stack([np.stack([c, s], -2), np.stack([-s, c], -2)], -3)


def inverse_complex(modes, live, length):
    a = angles(modes, length)
    c, s = np.cos(a) * live[..., None] / length, np.sin(a) * live[..., None] / length
    return np.stack([np.stack([c, -s], -2), np.stack([s, c], -2)], -3)


def contract_last(left, right):
    return lax.dot_general(
        left, right, (((1,), (1,)), ((), ())), precision=HIGHEST, preferred_element_type=jnp.float32
    )


def f32(a):
    return jnp.asarray(np.ascontiguousarray(a), jnp.float32)


def spectral(cotangent, rows, cols):
    nc, _, bx, by, nz = cotangent.shape
    nx, ny = bx * rows, by * cols
    mz, live_z = padded(np.arange(kept_modes(nz) + 1), cols)
    top_y = kept_modes(ny)
    my, live_y = padded(np.arange(-top_y, top_y + 1), rows)
    top_x = kept_modes(nx)
    mx = np.arange(-top_x, top_x + 1)
    kz, ky, kx = mz.shape[1], my.shape[1], len(mx)
    az = angles(mz, nz)
    table = np.stack([np.cos(az), -np.sin(az)], 1) * live_z[:, None, :, None]
    part = contract_last(f32(table.reshape(cols * 2 * kz, nz)), cotangent.reshape(nc * bx * by, nz))
    part = lax.all_to_all(part.reshape(cols, 2 * kz, nc * bx * by), "col", 0, 0)
    part = part.reshape(cols, 2, kz, nc, bx, by).transpose(2, 3, 4, 1, 0, 5)
    part = part.reshape(kz * nc * bx, 2 * ny)
    table = forward_complex(my, live_y, ny)
    table = table.transpose(0, 2, 1, 3, 4).reshape(rows * 2 * ky, 2 * ny)
    part = contract_last(f32(table), part)
    part = lax.all_to_all(part.reshape(rows, 2 * ky, kz * nc * bx), "row", 0, 0)
    part = part.reshape(rows, 2, ky, kz, nc, bx).transpose(4, 2, 3, 1, 0, 5)
    part = part.reshape(nc * ky * kz, 2 * nx)
    table = forward_complex(mx, np.ones(kx), nx)
    table = table.transpose(1, 0, 2, 3).reshape(2 * kx, 2 * nx)
    hat = contract_last(f32(table), part).reshape(2, kx, nc, ky * kz)
    wave_x = f32(mx)[:, None]
    wave_y = lax.dynamic_index_in_dim(f32(my), lax.axis_index("row"), 0, False)
    wave_z = lax.dynamic_index_in_dim(f32(mz), lax.axis_index("col"), 0, False)
    wave_y = jnp.broadcast_to(wave_y[:, None], (ky, kz)).reshape(1, ky * kz)
    wave_z = jnp.broadcast_to(wave_z[None, :], (ky, kz)).reshape(1, ky * kz)
    waves = [wave_x, wave_y, wave_z]
    vel = [hat[:, :, comp] for comp in range(3)]
    inner = waves[0] * vel[0] + waves[1] * vel[1] + waves[2] * vel[2]
    square = jnp.maximum(waves[0] * waves[0] + waves[1] * waves[1] + waves[2] * waves[2], 1.0)
    keep = (
        (3 * jnp.abs(waves[0]) < nx) & (3 * jnp.abs(waves[1]) < ny) & (3 * jnp.abs(waves[2]) < nz)
    )
    proj = [jnp.where(keep, vel[i] - waves[i] * inner / square, 0.0) for i in range(3)]
    sent = []
    for a, b in ((1, 1), (2, 2), (0, 1), (0, 2), (1, 2)):
        value = waves[a] * proj[a] if a == b else waves[b] * proj[a] + waves[a] * proj[b]
        sent.append(STEP_DT * value)
    ns = len(sent)
    part = jnp.stack(sent, axis=2).reshape(2 * kx, ns * ky * kz)
    table = inverse_complex(mx, np.ones(kx), nx)
    table = np.stack([table[:, :, 1], -table[:, :, 0]], 2)
    table = table.reshape(kx, 2, 2, rows, bx).transpose(3, 1, 4, 2, 0).reshape(rows * 2 * bx, 2 * kx)
    part = jnp.dot(f32(table), part, precision=HIGHEST, preferred_element_type=jnp.float32)
    part = lax.all_to_all(part.reshape(rows, 2 * bx, ns * ky * kz), "row", 0, 0)
    part = part.reshape(rows, 2, bx, ns, ky, kz).transpose(2, 3, 5, 1, 0, 4)
    part = part.reshape(bx * ns * kz, 2 * rows * ky)
    table = inverse_complex(my, live_y, ny)
    table = table.reshape(rows, ky, 2, 2, cols, by).transpose(4, 2, 5, 3, 0, 1)
    part = contract_last(f32(table.reshape(cols * 2 * by, 2 * rows * ky)), part)
    part = lax.all_to_all(part.reshape(cols, 2 * by, bx * ns * kz), "col", 0, 0)
    part = part.reshape(cols, 2, by, bx, ns, kz).transpose(4, 3, 2, 1, 0, 5)
    part = part.reshape(ns * bx * by, 2 * cols * kz)
    weight = np.where(mz == 0, 1.0, 2.0) * live_z / nz
    table = np.stack([np.cos(az), -np.sin(az)], 0) * weight[None, :, :, None]
    part = jnp.dot(
        part,
        f32(table.reshape(2 * cols * kz, nz)),
        precision=HIGHEST,
        preferred_element_type=jnp.float32,
    ).reshape(ns, bx * by * nz)
    return jnp.concatenate([-(part[0:1] + part[1:2]), part], axis=0)


def closure_kernel(steps, feat, s_ref, w1_ref, b1_ref, w2t_ref, w2_ref, b2_ref, wo_ref, wi_ref,
                   gx_ref, out_ref, left, accm, acci, acco):
    step = pl.program_id(0)
    hid = w2_ref.shape[0]
    ext = s_ref.shape[0]
    trans = (((1,), (1,)), ((), ()))

    @pl.when(step == 0)
    def _():
        accm[...] = jnp.zeros_like(accm)
        acci[...] = jnp.zeros_like(acci)
        acco[...] = jnp.zeros_like(acco)

    s = s_ref[...]
    left[pl.ds(hid, ext), :] = s
    pre = jnp.dot(w1_ref[...], s, preferred_element_type=jnp.float32) + b1_ref[...]
    act_in = jnp.tanh(pre).astype(jnp.bfloat16)
    left[pl.ds(0, hid), :] = act_in
    pre = jnp.dot(w2t_ref[...], act_in, preferred_element_type=jnp.float32) + b2_ref[...]
    act_mid = jnp.tanh(pre).astype(jnp.bfloat16)
    wide = act_mid.astype(jnp.float32)
    back = jnp.dot(wo_ref[...], s, preferred_element_type=jnp.float32)
    delta_mid = (back * (1.0 - wide * wide)).astype(jnp.bfloat16)
    acco[...] += lax.dot_general(s, act_mid, trans, preferred_element_type=jnp.float32)
    accm[...] += lax.dot_general(left[...], delta_mid, trans, preferred_element_type=jnp.float32)
    back = jnp.dot(w2_ref[...], delta_mid, preferred_element_type=jnp.float32)
    wide = left[pl.ds(0, hid), :].astype(jnp.float32)
    delta_in = (back * (1.0 - wide * wide)).astype(jnp.bfloat16)
    acci[...] += lax.dot_general(s, delta_in, trans, preferred_element_type=jnp.float32)
    grad = jnp.dot(wi_ref[...], delta_in, preferred_element_type=jnp.float32)
    gx_ref[...] = grad[:feat]

    @pl.when(step == steps - 1)
    def _():
        out_ref[...] = jnp.zeros_like(out_ref)
        out_ref[pl.ds(0, hid), :] = accm[pl.ds(0, hid), :]
        out_ref[pl.ds(hid, ext), :] = acci[...]
        row = lax.broadcasted_iota(jnp.int32, (ext, hid), 0)
        out_ref[pl.ds(hid + ext, ext), :] = jnp.where(
            row == feat, accm[pl.ds(hid, ext), :], acco[...]
        )


def closure(sources, feat, w_in, bias_in, w_mid, bias_mid, w_out, out_rows):
    ext, cells = sources.shape
    hid = w_mid.shape[0]
    block = math.gcd(cells, 2048)
    steps = cells // block
    outs = w_out.shape[1]
    w1 = jnp.concatenate([w_in.T, jnp.zeros((hid, ext - feat), jnp.bfloat16)], axis=1)
    wo = jnp.concatenate([jnp.zeros((hid, ext - outs), jnp.bfloat16), w_out], axis=1)
    wi = jnp.concatenate([w_in, jnp.zeros((ext - feat, hid), jnp.bfloat16)], axis=0)
    whole = lambda shape: pl.BlockSpec(shape, lambda i: (0, 0))
    return pl.pallas_call(
        functools.partial(closure_kernel, steps, feat),
        grid=(steps,),
        in_specs=[
            pl.BlockSpec((ext, block), lambda i: (0, i)),
            whole((hid, ext)),
            whole((hid, 1)),
            whole((hid, hid)),
            whole((hid, hid)),
            whole((hid, 1)),
            whole((hid, ext)),
            whole((ext, hid)),
        ],
        out_specs=[
            pl.BlockSpec((feat, block), lambda i: (0, i)),
            whole((out_rows, hid)),
        ],
        out_shape=[
            jax.ShapeDtypeStruct((feat, cells), jnp.float32),
            jax.ShapeDtypeStruct((out_rows, hid), jnp.float32),
        ],
        scratch_shapes=[
            pltpu.VMEM((hid + ext, block), jnp.bfloat16),
            pltpu.VMEM((hid + ext, hid), jnp.float32),
            pltpu.VMEM((ext, hid), jnp.float32),
            pltpu.VMEM((ext, hid), jnp.float32),
        ],
        compiler_params=pltpu.CompilerParams(vmem_limit_bytes=48 << 20),
        name="closure",
    )(sources, w1, bias_in[:, None], w_mid.T, w_mid, bias_mid[:, None], wo, wi)


def reduce_kernel(rows, cols, factor, g_ref, o_ref, rbuf, cbuf, send_r, recv_r, send_c, recv_c,
                  send_o, recv_o):
    me_r, me_c = lax.axis_index("row"), lax.axis_index("col")
    barrier = pltpu.get_barrier_semaphore()
    for d in range(1, rows):
        pl.semaphore_signal(
            barrier, inc=1, device_id=(lax.rem(me_r + d, rows), me_c), device_id_type=MESH
        )
    for d in range(1, cols):
        pl.semaphore_signal(
            barrier, inc=1, device_id=(me_r, lax.rem(me_c + d, cols)), device_id_type=MESH
        )
    pl.semaphore_wait(barrier, rows + cols - 2)
    first = []
    for d in range(1, rows):
        peer = lax.rem(me_r + d, rows)
        copy = pltpu.make_async_remote_copy(
            src_ref=g_ref.at[peer], dst_ref=rbuf.at[d], send_sem=send_r.at[d],
            recv_sem=recv_r.at[d], device_id=(peer, me_c), device_id_type=MESH,
        )
        copy.start()
        first.append(copy)
    total = g_ref[me_r]
    for d in range(1, rows):
        first[d - 1].wait_recv()
        total = total + rbuf[d]
    cbuf[me_c] = total
    second = []
    for d in range(1, cols):
        copy = pltpu.make_async_remote_copy(
            src_ref=cbuf.at[me_c], dst_ref=cbuf.at[me_c], send_sem=send_c.at[d],
            recv_sem=recv_c.at[d], device_id=(me_r, lax.rem(me_c + d, cols)), device_id_type=MESH,
        )
        copy.start()
        second.append(copy)
    for copy in second:
        copy.wait_recv()
    total = cbuf[0]
    for c in range(1, cols):
        total = total + cbuf[c]
    o_ref[me_r] = total * factor
    third = []
    for d in range(1, rows):
        copy = pltpu.make_async_remote_copy(
            src_ref=o_ref.at[me_r], dst_ref=o_ref.at[me_r], send_sem=send_o.at[d],
            recv_sem=recv_o.at[d], device_id=(lax.rem(me_r + d, rows), me_c), device_id_type=MESH,
        )
        copy.start()
        third.append(copy)
    for copy in third:
        copy.wait_recv()
    for copy in first + second + third:
        copy.wait_send()


def reduce_all(grads, rows, cols, factor):
    _, share, width = grads.shape
    dma = pltpu.SemaphoreType.DMA
    return pl.pallas_call(
        functools.partial(reduce_kernel, rows, cols, factor),
        out_shape=jax.ShapeDtypeStruct(grads.shape, jnp.float32),
        in_specs=[pl.BlockSpec(memory_space=pltpu.VMEM)],
        out_specs=pl.BlockSpec(memory_space=pltpu.VMEM),
        scratch_shapes=[
            pltpu.VMEM((rows, share, width), jnp.float32),
            pltpu.VMEM((cols, share, width), jnp.float32),
            dma((rows,)), dma((rows,)), dma((cols,)), dma((cols,)), dma((rows,)), dma((rows,)),
        ],
        compiler_params=pltpu.CompilerParams(collective_id=0, has_side_effects=True),
        name="reduce_all",
    )(grads)


def per_device(features, cotangent, w_in, bias_in, w_mid, bias_mid, w_out, rows, cols):
    stress = spectral(cotangent, rows, cols)
    feat, outs = features.shape[0], w_out.shape[1]
    hid = w_mid.shape[0]
    cells = math.prod(features.shape[1:])
    ext = 16 * (-(-(feat + 1 + outs) // 16))
    sources = jnp.concatenate(
        [
            features.reshape(feat, cells),
            jnp.ones((ext - feat - outs, cells), jnp.bfloat16),
            stress.astype(jnp.bfloat16),
        ],
        axis=0,
    )
    share = 8 * (-(-(hid + 2 * ext) // (8 * rows)))
    field, grads = closure(
        sources, feat, w_in, bias_in, w_mid, bias_mid, w_out, rows * share
    )
    factor = 1.0 / math.sqrt(cells * rows * cols)
    total = reduce_all(grads.reshape(rows, share, hid), rows, cols, factor)
    total = total.reshape(rows * share, hid)
    last = hid + ext
    return (
        field.reshape(features.shape),
        total[hid : hid + feat],
        total[hid + feat],
        total[:hid],
        total[last + feat],
        total[last + ext - outs : last + ext].T,
    )


def solution(mesh):
    body = functools.partial(per_device, rows=mesh.shape["row"], cols=mesh.shape["col"])
    return jax.shard_map(
        body,
        mesh=mesh,
        in_specs=(
            P(None, None, "row", "col", None),
            P(None, None, "row", "col", None),
            P(),
            P(),
            P(),
            P(),
            P(),
        ),
        out_specs=(P(None, None, "row", "col", None), P(), P(), P(), P(), P()),
        check_vma=False,
    )
```

```python
import functools
import math

import jax
import jax.numpy as jnp
import numpy as np
from jax import lax
from jax.experimental import pallas as pl
from jax.experimental.pallas import tpu as pltpu
from jax.sharding import PartitionSpec as P

STEP_DT = 0.04
MESH = pl.DeviceIdType.MESH
HIGHEST = lax.Precision.HIGHEST


def kept_modes(length):
    top = (length - 1) // 3
    return top


def padded(values, parts):
    share = -(-len(values) // parts)
    out = np.zeros((parts * share,), np.int64)
    out[: len(values)] = values
    live = np.zeros((parts * share,), np.float64)
    live[: len(values)] = 1.0
    return out.reshape(parts, share), live.reshape(parts, share)


def angles(modes, length):
    pos = np.arange(length)
    turns = (modes[..., None] * pos) % length
    return turns * (2.0 * math.pi / length)


def forward_complex(modes, live, length):
    a = angles(modes, length)
    c, s = np.cos(a) * live[..., None], np.sin(a) * live[..., None]
    return np.stack([np.stack([c, s], -2), np.stack([-s, c], -2)], -3)


def inverse_complex(modes, live, length):
    a = angles(modes, length)
    c, s = np.cos(a) * live[..., None] / length, np.sin(a) * live[..., None] / length
    return np.stack([np.stack([c, -s], -2), np.stack([s, c], -2)], -3)


def contract_last(left, right):
    return lax.dot_general(
        left, right, (((1,), (1,)), ((), ())), precision=HIGHEST, preferred_element_type=jnp.float32
    )


def f32(a):
    return jnp.asarray(np.ascontiguousarray(a), jnp.float32)


def exchange_kernel(axis, x_ref, o_ref, send, recv, local):
    me_r, me_c = lax.axis_index("row"), lax.axis_index("col")
    me = me_r if axis == "row" else me_c
    parts = x_ref.shape[0]

    def device(index):
        return (index, me_c) if axis == "row" else (me_r, index)

    barrier = pltpu.get_barrier_semaphore()
    for d in range(1, parts):
        pl.semaphore_signal(
            barrier, inc=1, device_id=device(lax.rem(me + d, parts)), device_id_type=MESH
        )
    own = pltpu.make_async_copy(x_ref.at[me], o_ref.at[me], local)
    own.start()
    pl.semaphore_wait(barrier, parts - 1)
    copies = []
    for d in range(1, parts):
        peer = lax.rem(me + d, parts)
        copy = pltpu.make_async_remote_copy(
            src_ref=x_ref.at[peer], dst_ref=o_ref.at[me], send_sem=send.at[d],
            recv_sem=recv.at[d], device_id=device(peer), device_id_type=MESH,
        )
        copy.start()
        copies.append(copy)
    own.wait()
    for copy in copies:
        copy.wait()


def exchange(x, axis, ident):
    parts = x.shape[0]
    dma = pltpu.SemaphoreType.DMA
    return pl.pallas_call(
        functools.partial(exchange_kernel, axis),
        out_shape=jax.ShapeDtypeStruct(x.shape, x.dtype),
        in_specs=[pl.BlockSpec(memory_space=pl.ANY)],
        out_specs=pl.BlockSpec(memory_space=pl.ANY),
        scratch_shapes=[dma((parts,)), dma((parts,)), dma(())],
        compiler_params=pltpu.CompilerParams(collective_id=ident, has_side_effects=True),
        name="exchange_" + axis,
    )(x)


def spectral(cotangent, rows, cols):
    nc, _, bx, by, nz = cotangent.shape
    nx, ny = bx * rows, by * cols
    mz, live_z = padded(np.arange(kept_modes(nz) + 1), cols)
    top_y = kept_modes(ny)
    my, live_y = padded(np.arange(-top_y, top_y + 1), rows)
    top_x = kept_modes(nx)
    mx = np.arange(-top_x, top_x + 1)
    kz, ky, kx = mz.shape[1], my.shape[1], len(mx)
    az = angles(mz, nz)
    table = np.stack([np.cos(az), -np.sin(az)], 1) * live_z[:, None, :, None]
    part = contract_last(f32(table.reshape(cols * 2 * kz, nz)), cotangent.reshape(nc * bx * by, nz))
    part = exchange(part.reshape(cols, 2 * kz, nc * bx * by), "col", 1)
    part = part.reshape(cols, 2, kz, nc, bx, by).transpose(2, 3, 4, 1, 0, 5)
    part = part.reshape(kz * nc * bx, 2 * ny)
    table = forward_complex(my, live_y, ny)
    table = table.transpose(0, 2, 1, 3, 4).reshape(rows * 2 * ky, 2 * ny)
    part = contract_last(f32(table), part)
    part = exchange(part.reshape(rows, 2 * ky, kz * nc * bx), "row", 2)
    part = part.reshape(rows, 2, ky, kz, nc, bx).transpose(4, 2, 3, 1, 0, 5)
    part = part.reshape(nc * ky * kz, 2 * nx)
    table = forward_complex(mx, np.ones(kx), nx)
    table = table.transpose(1, 0, 2, 3).reshape(2 * kx, 2 * nx)
    hat = contract_last(f32(table), part).reshape(2, kx, nc, ky * kz)
    wave_x = f32(mx)[:, None]
    wave_y = lax.dynamic_index_in_dim(f32(my), lax.axis_index("row"), 0, False)
    wave_z = lax.dynamic_index_in_dim(f32(mz), lax.axis_index("col"), 0, False)
    wave_y = jnp.broadcast_to(wave_y[:, None], (ky, kz)).reshape(1, ky * kz)
    wave_z = jnp.broadcast_to(wave_z[None, :], (ky, kz)).reshape(1, ky * kz)
    waves = [wave_x, wave_y, wave_z]
    vel = [hat[:, :, comp] for comp in range(3)]
    inner = waves[0] * vel[0] + waves[1] * vel[1] + waves[2] * vel[2]
    square = jnp.maximum(waves[0] * waves[0] + waves[1] * waves[1] + waves[2] * waves[2], 1.0)
    keep = (
        (3 * jnp.abs(waves[0]) < nx) & (3 * jnp.abs(waves[1]) < ny) & (3 * jnp.abs(waves[2]) < nz)
    )
    proj = [jnp.where(keep, vel[i] - waves[i] * inner / square, 0.0) for i in range(3)]
    sent = []
    for a, b in ((1, 1), (2, 2), (0, 1), (0, 2), (1, 2)):
        value = waves[a] * proj[a] if a == b else waves[b] * proj[a] + waves[a] * proj[b]
        sent.append((STEP_DT * value).reshape(2 * kx, ky, kz))
    ns = len(sent)
    wide = 2 ** math.ceil(math.log2(ns * kz))
    part = jnp.concatenate(sent + [jnp.zeros((2 * kx, ky, wide - ns * kz), jnp.float32)], axis=2)
    part = part.reshape(2 * kx, ky * wide)
    table = inverse_complex(mx, np.ones(kx), nx)
    table = np.stack([table[:, :, 1], -table[:, :, 0]], 2)
    table = table.reshape(kx, 2, 2, rows, bx).transpose(3, 1, 4, 2, 0).reshape(rows * 2 * bx, 2 * kx)
    part = jnp.dot(f32(table), part, precision=HIGHEST, preferred_element_type=jnp.float32)
    part = exchange(part.reshape(rows, 2 * bx, ky * wide), "row", 3)
    part = part.reshape(rows * 2, bx, ky, wide).transpose(0, 2, 1, 3)
    part = part.reshape(rows * 2 * ky, bx * wide)
    table = inverse_complex(my, live_y, ny)
    table = table.reshape(rows, ky, 2, 2, cols, by).transpose(4, 2, 5, 0, 3, 1)
    table = f32(table.reshape(cols * 2 * by, rows * 2 * ky))
    part = jnp.dot(table, part, precision=HIGHEST, preferred_element_type=jnp.float32)
    part = exchange(part.reshape(cols, 2 * by, bx * wide), "col", 4)
    part = part.reshape(cols * 2, by, bx, wide).transpose(2, 1, 0, 3)
    part = part.reshape(bx * by, cols * 2 * wide)
    weight = np.where(mz == 0, 1.0, 2.0) * live_z / nz
    table = np.stack([np.cos(az), -np.sin(az)], 1) * weight[:, None, :, None]
    full = np.zeros((cols, 2, wide, ns + 1, nz))
    for comp in range(ns):
        full[:, :, comp * kz : (comp + 1) * kz, comp + 1] = table
    full[:, :, :, 0] = -(full[:, :, :, 1] + full[:, :, :, 2])
    part = jnp.dot(
        part,
        f32(full.reshape(cols * 2 * wide, (ns + 1) * nz)),
        precision=HIGHEST,
        preferred_element_type=jnp.float32,
    )
    return part.reshape(bx * by, ns + 1, nz).transpose(1, 0, 2).reshape(ns + 1, bx * by * nz)


def closure_kernel(steps, feat, s_ref, w1_ref, b1_ref, w2t_ref, w2_ref, b2_ref, wo_ref, wi_ref,
                   gx_ref, out_ref, accm, acci, acco, accb):
    step = pl.program_id(0)
    hid = w2_ref.shape[0]
    ext = s_ref.shape[0]
    first = (((0,), (0,)), ((), ()))
    last = (((1,), (1,)), ((), ()))

    @pl.when(step == 0)
    def _():
        accm[...] = jnp.zeros_like(accm)
        acci[...] = jnp.zeros_like(acci)
        acco[...] = jnp.zeros_like(acco)
        accb[...] = jnp.zeros_like(accb)

    s = s_ref[...]
    pre = lax.dot_general(s, w1_ref[...], first, preferred_element_type=jnp.float32) + b1_ref[...]
    act_in = jnp.tanh(pre).astype(jnp.bfloat16)
    pre = jnp.dot(act_in, w2_ref[...], preferred_element_type=jnp.float32) + b2_ref[...]
    act_mid = jnp.tanh(pre).astype(jnp.bfloat16)
    wide = act_mid.astype(jnp.float32)
    back = lax.dot_general(s, wo_ref[...], first, preferred_element_type=jnp.float32)
    delta_mid = (back * (1.0 - wide * wide)).astype(jnp.bfloat16)
    accb[...] += jnp.sum(delta_mid.astype(jnp.float32), axis=0, keepdims=True)
    acco[...] += jnp.dot(s, act_mid, preferred_element_type=jnp.float32)
    accm[...] += lax.dot_general(act_in, delta_mid, first, preferred_element_type=jnp.float32)
    back = jnp.dot(delta_mid, w2t_ref[...], preferred_element_type=jnp.float32)
    wide = act_in.astype(jnp.float32)
    delta_in = (back * (1.0 - wide * wide)).astype(jnp.bfloat16)
    acci[...] += jnp.dot(s, delta_in, preferred_element_type=jnp.float32)
    grad = lax.dot_general(wi_ref[...], delta_in, last, preferred_element_type=jnp.float32)
    gx_ref[...] = grad[:feat]

    @pl.when(step == steps - 1)
    def _():
        out_ref[...] = jnp.zeros_like(out_ref)
        out_ref[pl.ds(0, hid), :] = accm[...]
        out_ref[pl.ds(hid, ext), :] = acci[...]
        row = lax.broadcasted_iota(jnp.int32, (ext, hid), 0)
        out_ref[pl.ds(hid + ext, ext), :] = jnp.where(row == feat, accb[...], acco[...])


def closure(sources, feat, w_in, bias_in, w_mid, bias_mid, w_out, out_rows):
    ext, cells = sources.shape
    hid = w_mid.shape[0]
    block = math.gcd(cells, 4096)
    steps = cells // block
    outs = w_out.shape[1]
    wi = jnp.concatenate([w_in, jnp.zeros((ext - feat, hid), jnp.bfloat16)], axis=0)
    wo = jnp.concatenate([jnp.zeros((ext - outs, hid), jnp.bfloat16), w_out.T], axis=0)
    whole = lambda shape: pl.BlockSpec(shape, lambda i: (0, 0))
    return pl.pallas_call(
        functools.partial(closure_kernel, steps, feat),
        grid=(steps,),
        in_specs=[
            pl.BlockSpec((ext, block), lambda i: (0, i)),
            whole((ext, hid)),
            whole((1, hid)),
            whole((hid, hid)),
            whole((hid, hid)),
            whole((1, hid)),
            whole((ext, hid)),
            whole((ext, hid)),
        ],
        out_specs=[
            pl.BlockSpec((feat, block), lambda i: (0, i)),
            whole((out_rows, hid)),
        ],
        out_shape=[
            jax.ShapeDtypeStruct((feat, cells), jnp.float32),
            jax.ShapeDtypeStruct((out_rows, hid), jnp.float32),
        ],
        scratch_shapes=[
            pltpu.VMEM((hid, hid), jnp.float32),
            pltpu.VMEM((ext, hid), jnp.float32),
            pltpu.VMEM((ext, hid), jnp.float32),
            pltpu.VMEM((1, hid), jnp.float32),
        ],
        compiler_params=pltpu.CompilerParams(vmem_limit_bytes=48 << 20),
        name="closure",
    )(sources, wi, bias_in[None], w_mid.T, w_mid, bias_mid[None], wo, wi)


def reduce_kernel(rows, cols, factor, g_ref, o_ref, rbuf, cbuf, send_r, recv_r, send_c, recv_c,
                  send_o, recv_o):
    me_r, me_c = lax.axis_index("row"), lax.axis_index("col")
    barrier = pltpu.get_barrier_semaphore()
    for d in range(1, rows):
        pl.semaphore_signal(
            barrier, inc=1, device_id=(lax.rem(me_r + d, rows), me_c), device_id_type=MESH
        )
    for d in range(1, cols):
        pl.semaphore_signal(
            barrier, inc=1, device_id=(me_r, lax.rem(me_c + d, cols)), device_id_type=MESH
        )
    pl.semaphore_wait(barrier, rows + cols - 2)
    first = []
    for d in range(1, rows):
        peer = lax.rem(me_r + d, rows)
        copy = pltpu.make_async_remote_copy(
            src_ref=g_ref.at[peer], dst_ref=rbuf.at[d], send_sem=send_r.at[d],
            recv_sem=recv_r.at[d], device_id=(peer, me_c), device_id_type=MESH,
        )
        copy.start()
        first.append(copy)
    total = g_ref[me_r]
    for d in range(1, rows):
        first[d - 1].wait_recv()
        total = total + rbuf[d]
    cbuf[me_c] = total
    second = []
    for d in range(1, cols):
        copy = pltpu.make_async_remote_copy(
            src_ref=cbuf.at[me_c], dst_ref=cbuf.at[me_c], send_sem=send_c.at[d],
            recv_sem=recv_c.at[d], device_id=(me_r, lax.rem(me_c + d, cols)), device_id_type=MESH,
        )
        copy.start()
        second.append(copy)
    for copy in second:
        copy.wait_recv()
    total = cbuf[0]
    for c in range(1, cols):
        total = total + cbuf[c]
    o_ref[me_r] = total * factor
    third = []
    for d in range(1, rows):
        copy = pltpu.make_async_remote_copy(
            src_ref=o_ref.at[me_r], dst_ref=o_ref.at[me_r], send_sem=send_o.at[d],
            recv_sem=recv_o.at[d], device_id=(lax.rem(me_r + d, rows), me_c), device_id_type=MESH,
        )
        copy.start()
        third.append(copy)
    for copy in third:
        copy.wait_recv()
    for copy in first + second + third:
        copy.wait_send()


def reduce_all(grads, rows, cols, factor):
    _, share, width = grads.shape
    dma = pltpu.SemaphoreType.DMA
    return pl.pallas_call(
        functools.partial(reduce_kernel, rows, cols, factor),
        out_shape=jax.ShapeDtypeStruct(grads.shape, jnp.float32),
        in_specs=[pl.BlockSpec(memory_space=pltpu.VMEM)],
        out_specs=pl.BlockSpec(memory_space=pltpu.VMEM),
        scratch_shapes=[
            pltpu.VMEM((rows, share, width), jnp.float32),
            pltpu.VMEM((cols, share, width), jnp.float32),
            dma((rows,)), dma((rows,)), dma((cols,)), dma((cols,)), dma((rows,)), dma((rows,)),
        ],
        compiler_params=pltpu.CompilerParams(collective_id=0, has_side_effects=True),
        name="reduce_all",
    )(grads)


def per_device(features, cotangent, w_in, bias_in, w_mid, bias_mid, w_out, rows, cols):
    stress = spectral(cotangent, rows, cols)
    feat, outs = features.shape[0], w_out.shape[1]
    hid = w_mid.shape[0]
    cells = math.prod(features.shape[1:])
    ext = 16 * (-(-(feat + 1 + outs) // 16))
    sources = jnp.concatenate(
        [
            features.reshape(feat, cells),
            jnp.ones((ext - feat - outs, cells), jnp.bfloat16),
            stress.astype(jnp.bfloat16),
        ],
        axis=0,
    )
    share = 8 * (-(-(hid + 2 * ext) // (8 * rows)))
    field, grads = closure(
        sources, feat, w_in, bias_in, w_mid, bias_mid, w_out, rows * share
    )
    factor = 1.0 / math.sqrt(cells * rows * cols)
    total = reduce_all(grads.reshape(rows, share, hid), rows, cols, factor)
    total = total.reshape(rows * share, hid)
    last = hid + ext
    return (
        field.reshape(features.shape),
        total[hid : hid + feat],
        total[hid + feat],
        total[:hid],
        total[last + feat],
        total[last + ext - outs : last + ext].T,
    )


def solution(mesh):
    body = functools.partial(per_device, rows=mesh.shape["row"], cols=mesh.shape["col"])
    return jax.shard_map(
        body,
        mesh=mesh,
        in_specs=(
            P(None, None, "row", "col", None),
            P(None, None, "row", "col", None),
            P(),
            P(),
            P(),
            P(),
            P(),
        ),
        out_specs=(P(None, None, "row", "col", None), P(), P(), P(), P(), P()),
        check_vma=False,
    )
```

```python
import functools
import math

import jax
import jax.numpy as jnp
import numpy as np
from jax import lax
from jax.experimental import pallas as pl
from jax.experimental.pallas import tpu as pltpu
from jax.sharding import PartitionSpec as P

STEP_DT = 0.04
MESH = pl.DeviceIdType.MESH
HIGHEST = lax.Precision.HIGHEST


def kept_modes(length):
    top = (length - 1) // 3
    return top


def padded(values, parts):
    share = -(-len(values) // parts)
    out = np.zeros((parts * share,), np.int64)
    out[: len(values)] = values
    live = np.zeros((parts * share,), np.float64)
    live[: len(values)] = 1.0
    return out.reshape(parts, share), live.reshape(parts, share)


def angles(modes, length):
    pos = np.arange(length)
    turns = (modes[..., None] * pos) % length
    return turns * (2.0 * math.pi / length)


def forward_complex(modes, live, length):
    a = angles(modes, length)
    c, s = np.cos(a) * live[..., None], np.sin(a) * live[..., None]
    return np.stack([np.stack([c, s], -2), np.stack([-s, c], -2)], -3)


def inverse_complex(modes, live, length):
    a = angles(modes, length)
    c, s = np.cos(a) * live[..., None] / length, np.sin(a) * live[..., None] / length
    return np.stack([np.stack([c, -s], -2), np.stack([s, c], -2)], -3)


def contract_last(left, right):
    return lax.dot_general(
        left, right, (((1,), (1,)), ((), ())), precision=HIGHEST, preferred_element_type=jnp.float32
    )


def f32(a):
    return jnp.asarray(np.ascontiguousarray(a), jnp.float32)


def exchange_kernel(axis, x_ref, o_ref, send, recv, local):
    me_r, me_c = lax.axis_index("row"), lax.axis_index("col")
    me = me_r if axis == "row" else me_c
    parts = x_ref.shape[0]

    def device(index):
        return (index, me_c) if axis == "row" else (me_r, index)

    barrier = pltpu.get_barrier_semaphore()
    for d in range(1, parts):
        pl.semaphore_signal(
            barrier, inc=1, device_id=device(lax.rem(me + d, parts)), device_id_type=MESH
        )
    own = pltpu.make_async_copy(x_ref.at[me], o_ref.at[me], local)
    own.start()
    pl.semaphore_wait(barrier, parts - 1)
    copies = []
    for d in range(1, parts):
        peer = lax.rem(me + d, parts)
        copy = pltpu.make_async_remote_copy(
            src_ref=x_ref.at[peer], dst_ref=o_ref.at[me], send_sem=send.at[d],
            recv_sem=recv.at[d], device_id=device(peer), device_id_type=MESH,
        )
        copy.start()
        copies.append(copy)
    own.wait()
    for copy in copies:
        copy.wait()


def exchange(x, axis, ident):
    parts = x.shape[0]
    dma = pltpu.SemaphoreType.DMA
    return pl.pallas_call(
        functools.partial(exchange_kernel, axis),
        out_shape=jax.ShapeDtypeStruct(x.shape, x.dtype),
        in_specs=[pl.BlockSpec(memory_space=pl.ANY)],
        out_specs=pl.BlockSpec(memory_space=pl.ANY),
        scratch_shapes=[dma((parts,)), dma((parts,)), dma(())],
        compiler_params=pltpu.CompilerParams(collective_id=ident, has_side_effects=True),
        name="exchange_" + axis,
    )(x)


def spectral(cotangent, rows, cols):
    nc, _, bx, by, nz = cotangent.shape
    nx, ny = bx * rows, by * cols
    mz, live_z = padded(np.arange(kept_modes(nz) + 1), cols)
    top_y = kept_modes(ny)
    my, live_y = padded(np.arange(-top_y, top_y + 1), rows)
    top_x = kept_modes(nx)
    mx = np.arange(-top_x, top_x + 1)
    kz, ky, kx = mz.shape[1], my.shape[1], len(mx)
    az = angles(mz, nz)
    table = np.stack([np.cos(az), -np.sin(az)], 1) * live_z[:, None, :, None]
    part = contract_last(f32(table.reshape(cols * 2 * kz, nz)), cotangent.reshape(nc * bx * by, nz))
    part = exchange(part.reshape(cols, 2 * kz, nc * bx * by), "col", 1)
    part = part.reshape(cols, 2, kz, nc, bx, by).transpose(2, 3, 4, 1, 0, 5)
    part = part.reshape(kz * nc * bx, 2 * ny)
    table = forward_complex(my, live_y, ny)
    table = table.transpose(0, 2, 1, 3, 4).reshape(rows * 2 * ky, 2 * ny)
    part = contract_last(f32(table), part)
    part = exchange(part.reshape(rows, 2 * ky, kz * nc * bx), "row", 2)
    part = part.reshape(rows, 2, ky, kz, nc, bx).transpose(4, 2, 3, 1, 0, 5)
    part = part.reshape(nc * ky * kz, 2 * nx)
    table = forward_complex(mx, np.ones(kx), nx)
    table = table.transpose(1, 0, 2, 3).reshape(2 * kx, 2 * nx)
    hat = contract_last(f32(table), part).reshape(2, kx, nc, ky * kz)
    wave_x = f32(mx)[:, None]
    wave_y = lax.dynamic_index_in_dim(f32(my), lax.axis_index("row"), 0, False)
    wave_z = lax.dynamic_index_in_dim(f32(mz), lax.axis_index("col"), 0, False)
    wave_y = jnp.broadcast_to(wave_y[:, None], (ky, kz)).reshape(1, ky * kz)
    wave_z = jnp.broadcast_to(wave_z[None, :], (ky, kz)).reshape(1, ky * kz)
    waves = [wave_x, wave_y, wave_z]
    vel = [hat[:, :, comp] for comp in range(3)]
    inner = waves[0] * vel[0] + waves[1] * vel[1] + waves[2] * vel[2]
    square = jnp.maximum(waves[0] * waves[0] + waves[1] * waves[1] + waves[2] * waves[2], 1.0)
    proj = [vel[i] - waves[i] * inner / square for i in range(3)]
    sent = []
    for a, b in ((1, 1), (2, 2), (0, 1), (0, 2), (1, 2)):
        value = waves[a] * proj[a] if a == b else waves[b] * proj[a] + waves[a] * proj[b]
        sent.append((STEP_DT * value).reshape(2 * kx, ky, kz))
    ns = len(sent)
    wide = 8 * (-(-(ns * kz) // 8))
    part = jnp.concatenate(sent + [jnp.zeros((2 * kx, ky, wide - ns * kz), jnp.float32)], axis=2)
    part = part.reshape(2 * kx, ky * wide)
    table = inverse_complex(mx, np.ones(kx), nx)
    table = np.stack([table[:, :, 1], -table[:, :, 0]], 2)
    table = table.reshape(kx, 2, 2, rows, bx).transpose(3, 1, 4, 2, 0).reshape(rows * 2 * bx, 2 * kx)
    part = jnp.dot(f32(table), part, precision=HIGHEST, preferred_element_type=jnp.float32)
    part = exchange(part.reshape(rows, 2 * bx, ky * wide), "row", 3)
    part = part.reshape(rows * 2, bx, ky, wide).transpose(0, 2, 1, 3)
    part = part.reshape(rows * 2 * ky, bx * wide)
    table = inverse_complex(my, live_y, ny)
    table = table.reshape(rows, ky, 2, 2, cols, by).transpose(4, 2, 5, 0, 3, 1)
    table = f32(table.reshape(cols * 2 * by, rows * 2 * ky))
    part = jnp.dot(table, part, precision=HIGHEST, preferred_element_type=jnp.float32)
    part = exchange(part.reshape(cols, 2 * by, bx * wide), "col", 4)
    part = part.reshape(cols * 2, by, bx, wide).transpose(2, 1, 0, 3)
    part = part.reshape(bx * by, cols * 2 * wide)
    weight = np.where(mz == 0, 1.0, 2.0) * live_z / nz
    table = np.stack([np.cos(az), -np.sin(az)], 1) * weight[:, None, :, None]
    full = np.zeros((cols, 2, wide, ns + 1, nz))
    for comp in range(ns):
        full[:, :, comp * kz : (comp + 1) * kz, comp + 1] = table
    full[:, :, :, 0] = -(full[:, :, :, 1] + full[:, :, :, 2])
    part = jnp.dot(
        part,
        f32(full.reshape(cols * 2 * wide, (ns + 1) * nz)),
        precision=HIGHEST,
        preferred_element_type=jnp.float32,
    )
    return part.reshape(bx * by, ns + 1, nz).transpose(1, 0, 2).reshape(ns + 1, bx * by * nz)


def closure_kernel(steps, feat, s_ref, w1_ref, b1_ref, w2t_ref, w2_ref, b2_ref, wo_ref, wi_ref,
                   gx_ref, out_ref, accm, acci, acco, accb):
    step = pl.program_id(0)
    hid = w2_ref.shape[0]
    ext = s_ref.shape[0]
    first = (((0,), (0,)), ((), ()))
    last = (((1,), (1,)), ((), ()))

    @pl.when(step == 0)
    def _():
        accm[...] = jnp.zeros_like(accm)
        acci[...] = jnp.zeros_like(acci)
        acco[...] = jnp.zeros_like(acco)
        accb[...] = jnp.zeros_like(accb)

    s = s_ref[...]
    pre = lax.dot_general(s, w1_ref[...], first, preferred_element_type=jnp.float32) + b1_ref[...]
    act_in = jnp.tanh(pre).astype(jnp.bfloat16)
    pre = jnp.dot(act_in, w2_ref[...], preferred_element_type=jnp.float32) + b2_ref[...]
    act_mid = jnp.tanh(pre).astype(jnp.bfloat16)
    wide = act_mid.astype(jnp.float32)
    back = lax.dot_general(s, wo_ref[...], first, preferred_element_type=jnp.float32)
    delta_mid = (back * (1.0 - wide * wide)).astype(jnp.bfloat16)
    accb[...] += jnp.sum(delta_mid.astype(jnp.float32), axis=0, keepdims=True)
    acco[...] += jnp.dot(s, act_mid, preferred_element_type=jnp.float32)
    accm[...] += lax.dot_general(act_in, delta_mid, first, preferred_element_type=jnp.float32)
    back = jnp.dot(delta_mid, w2t_ref[...], preferred_element_type=jnp.float32)
    wide = act_in.astype(jnp.float32)
    delta_in = (back * (1.0 - wide * wide)).astype(jnp.bfloat16)
    acci[...] += jnp.dot(s, delta_in, preferred_element_type=jnp.float32)
    grad = lax.dot_general(wi_ref[...], delta_in, last, preferred_element_type=jnp.float32)
    for row in range(gx_ref.shape[1]):
        gx_ref[:, row, :] = grad[:feat, row * 128 : (row + 1) * 128]

    @pl.when(step == steps - 1)
    def _():
        out_ref[...] = jnp.zeros_like(out_ref)
        out_ref[pl.ds(0, hid), :] = accm[...]
        out_ref[pl.ds(hid, ext), :] = acci[...]
        row = lax.broadcasted_iota(jnp.int32, (ext, hid), 0)
        out_ref[pl.ds(hid + ext, ext), :] = jnp.where(row == feat, accb[...], acco[...])


def closure(sources, feat, w_in, bias_in, w_mid, bias_mid, w_out, out_rows):
    ext, cells = sources.shape
    hid = w_mid.shape[0]
    block = math.gcd(cells, 4096)
    steps = cells // block
    outs = w_out.shape[1]
    wi = jnp.concatenate([w_in, jnp.zeros((ext - feat, hid), jnp.bfloat16)], axis=0)
    wo = jnp.concatenate([jnp.zeros((ext - outs, hid), jnp.bfloat16), w_out.T], axis=0)
    whole = lambda shape: pl.BlockSpec(shape, lambda i: (0, 0))
    return pl.pallas_call(
        functools.partial(closure_kernel, steps, feat),
        grid=(steps,),
        in_specs=[
            pl.BlockSpec((ext, block), lambda i: (0, i)),
            whole((ext, hid)),
            whole((1, hid)),
            whole((hid, hid)),
            whole((hid, hid)),
            whole((1, hid)),
            whole((ext, hid)),
            whole((ext, hid)),
        ],
        out_specs=[
            pl.BlockSpec((feat, block // 128, 128), lambda i: (0, i, 0)),
            whole((out_rows, hid)),
        ],
        out_shape=[
            jax.ShapeDtypeStruct((feat, cells // 128, 128), jnp.float32),
            jax.ShapeDtypeStruct((out_rows, hid), jnp.float32),
        ],
        scratch_shapes=[
            pltpu.VMEM((hid, hid), jnp.float32),
            pltpu.VMEM((ext, hid), jnp.float32),
            pltpu.VMEM((ext, hid), jnp.float32),
            pltpu.VMEM((1, hid), jnp.float32),
        ],
        compiler_params=pltpu.CompilerParams(vmem_limit_bytes=48 << 20),
        name="closure",
    )(sources, wi, bias_in[None], w_mid.T, w_mid, bias_mid[None], wo, wi)


def reduce_kernel(rows, cols, factor, g_ref, o_ref, rbuf, cbuf, send_r, recv_r, send_c, recv_c,
                  send_o, recv_o):
    me_r, me_c = lax.axis_index("row"), lax.axis_index("col")
    barrier = pltpu.get_barrier_semaphore()
    for d in range(1, rows):
        pl.semaphore_signal(
            barrier, inc=1, device_id=(lax.rem(me_r + d, rows), me_c), device_id_type=MESH
        )
    for d in range(1, cols):
        pl.semaphore_signal(
            barrier, inc=1, device_id=(me_r, lax.rem(me_c + d, cols)), device_id_type=MESH
        )
    pl.semaphore_wait(barrier, rows + cols - 2)
    first = []
    for d in range(1, rows):
        peer = lax.rem(me_r + d, rows)
        copy = pltpu.make_async_remote_copy(
            src_ref=g_ref.at[peer], dst_ref=rbuf.at[d], send_sem=send_r.at[d],
            recv_sem=recv_r.at[d], device_id=(peer, me_c), device_id_type=MESH,
        )
        copy.start()
        first.append(copy)
    total = g_ref[me_r]
    for d in range(1, rows):
        first[d - 1].wait_recv()
        total = total + rbuf[d]
    cbuf[me_c] = total
    second = []
    for d in range(1, cols):
        copy = pltpu.make_async_remote_copy(
            src_ref=cbuf.at[me_c], dst_ref=cbuf.at[me_c], send_sem=send_c.at[d],
            recv_sem=recv_c.at[d], device_id=(me_r, lax.rem(me_c + d, cols)), device_id_type=MESH,
        )
        copy.start()
        second.append(copy)
    for copy in second:
        copy.wait_recv()
    total = cbuf[0]
    for c in range(1, cols):
        total = total + cbuf[c]
    o_ref[me_r] = total * factor
    third = []
    for d in range(1, rows):
        copy = pltpu.make_async_remote_copy(
            src_ref=o_ref.at[me_r], dst_ref=o_ref.at[me_r], send_sem=send_o.at[d],
            recv_sem=recv_o.at[d], device_id=(lax.rem(me_r + d, rows), me_c), device_id_type=MESH,
        )
        copy.start()
        third.append(copy)
    for copy in third:
        copy.wait_recv()
    for copy in first + second + third:
        copy.wait_send()


def reduce_all(grads, rows, cols, factor):
    _, share, width = grads.shape
    dma = pltpu.SemaphoreType.DMA
    return pl.pallas_call(
        functools.partial(reduce_kernel, rows, cols, factor),
        out_shape=jax.ShapeDtypeStruct(grads.shape, jnp.float32),
        in_specs=[pl.BlockSpec(memory_space=pltpu.VMEM)],
        out_specs=pl.BlockSpec(memory_space=pltpu.VMEM),
        scratch_shapes=[
            pltpu.VMEM((rows, share, width), jnp.float32),
            pltpu.VMEM((cols, share, width), jnp.float32),
            dma((rows,)), dma((rows,)), dma((cols,)), dma((cols,)), dma((rows,)), dma((rows,)),
        ],
        compiler_params=pltpu.CompilerParams(collective_id=0, has_side_effects=True),
        name="reduce_all",
    )(grads)


def per_device(features, cotangent, w_in, bias_in, w_mid, bias_mid, w_out, rows, cols):
    stress = spectral(cotangent, rows, cols)
    feat, outs = features.shape[0], w_out.shape[1]
    hid = w_mid.shape[0]
    cells = math.prod(features.shape[1:])
    ext = 16 * (-(-(feat + 1 + outs) // 16))
    sources = jnp.concatenate(
        [
            features.reshape(feat, cells),
            jnp.ones((ext - feat - outs, cells), jnp.bfloat16),
            stress.astype(jnp.bfloat16),
        ],
        axis=0,
    )
    share = 8 * (-(-(hid + 2 * ext) // (8 * rows)))
    field, grads = closure(
        sources, feat, w_in, bias_in, w_mid, bias_mid, w_out, rows * share
    )
    factor = 1.0 / math.sqrt(cells * rows * cols)
    total = reduce_all(grads.reshape(rows, share, hid), rows, cols, factor)
    total = total.reshape(rows * share, hid)
    last = hid + ext
    return (
        field.reshape(features.shape),
        total[hid : hid + feat],
        total[hid + feat],
        total[:hid],
        total[last + feat],
        total[last + ext - outs : last + ext].T,
    )


def solution(mesh):
    body = functools.partial(per_device, rows=mesh.shape["row"], cols=mesh.shape["col"])
    return jax.shard_map(
        body,
        mesh=mesh,
        in_specs=(
            P(None, None, "row", "col", None),
            P(None, None, "row", "col", None),
            P(),
            P(),
            P(),
            P(),
            P(),
        ),
        out_specs=(P(None, None, "row", "col", None), P(), P(), P(), P(), P()),
        check_vma=False,
    )
```
